512 devices in a mesh: ctx: 32 (over x, y), head: 16 (over z, core).
Axes of the slice: x: 4, y: 8, z: 8, core: 2. Of those that a mesh axis runs over, the one named last changes fastest.
Arguments:
- queries: bfloat16 [32768, 4096], P('ctx', 'head'), may hold values from -2.5 to 2.5
- key_vectors: bfloat16 [32768, 4096], P('ctx', 'head'), may hold values from -2.5 to 2.5
- value_vectors: bfloat16 [32768, 4096], P('ctx', 'head'), may hold values from -24 to 24
- out_grad: bfloat16 [32768, 4096], P('ctx', 'head'), may hold values from -6 to 6
- norm_gain: float32 [4096], P('head'), may hold values from 0.1 to 1.9
Outputs:
- query_grad: bfloat16 [32768, 4096], P('ctx', 'head')
- key_grad: bfloat16 [32768, 4096], P('ctx', 'head')
- value_grad: bfloat16 [32768, 4096], P('ctx', 'head')
The draws below stay inside these ranges and needn't reach their ends.
All inputs are finite; a program needn't handle non-finite values.
Results may differ from the reference program's by a relative error of at most 0.0058.
Values sent between devices are 32-bit elements; how exact they have to be, the bound alone decides.
A program may use at most 64 MiB of HBM per device.

```python
import jax
import jax.numpy as jnp
from jax import lax

HD = 128
BLOCK = 512
HEADS = 32
TOKENS = 32768


def draw_value_vectors(key, part):
    key_normal, key_head, key_column = jax.random.split(key, 3)
    head_pos = jnp.arange(HEADS, dtype=jnp.float32) / max(HEADS - 1, 1)
    head_scale = (10.0 ** head_pos)[:, None] * jnp.exp(jax.random.uniform(key_head, (HEADS, 1), jnp.float32, -0.2, 0.2))
    column_scale = jnp.exp(jax.random.uniform(key_column, (HEADS, HD), jnp.float32, -0.35, 0.35))
    normal_part = jnp.clip(jax.random.normal(key_normal, (TOKENS, HEADS, HD), jnp.float32), -4.0, 4.0)
    drawn = 0.3 * normal_part * head_scale[None] * column_scale[None]
    return drawn.reshape(TOKENS, HEADS * HD).astype(jnp.bfloat16)


def level_of(rng, shape, cuts, least, high):
    def one(axis_at, parts):
        draws = jax.random.uniform(jax.random.fold_in(jax.random.fold_in(rng, 6), axis_at), (parts,), jnp.float32, least / len(cuts), high / len(cuts))
        return jnp.repeat(jnp.exp(draws), shape[axis_at] // parts).reshape((-1,) + (1,) * (len(shape) - axis_at - 1))

    level = one(*cuts[0])
    for cut in cuts[1:]:
        level = level * one(*cut)
    return level


def scatter_about(stream_key, extent, scale, most, cuts=(), held_as=jnp.bfloat16):
    loudness = level_of(stream_key, extent, cuts, -0.22, 0.18) if cuts else 1.0
    entries = jax.random.normal(stream_key, extent, jnp.float32) * scale * loudness
    return jnp.minimum(jnp.maximum(entries, -most), most).astype(held_as)


def setup_inputs(seed: int = 0) -> dict:
    arg_keys = jax.random.split(jax.random.key(seed), 6)
    return {
        "queries": scatter_about(arg_keys[0], (TOKENS, HEADS * HD), 0.3, 2.5, ((0, 32), (1, 16))),
        "key_vectors": scatter_about(arg_keys[1], (TOKENS, HEADS * HD), 0.3, 2.5, ((0, 32), (1, 16))),
        "value_vectors": draw_value_vectors(jax.random.fold_in(arg_keys[5], 71), 0),
        "out_grad": scatter_about(arg_keys[3], (TOKENS, HEADS * HD), 1.0, 6.0, ((0, 32), (1, 16))),
        "norm_gain": jnp.clip(1.0 + 0.18 * jax.random.normal(arg_keys[4], (HEADS * HD,), jnp.float32), 0.1, 1.9),
    }


epsilon = 1e-05

def rounded(matrix):
    return lax.optimization_barrier(matrix.astype(jnp.bfloat16))

def lower_mask():
    positions = jnp.arange(BLOCK, dtype=jnp.int32)
    return positions[:, None] >= positions[None, :]

def reference(queries, key_vectors, value_vectors, out_grad, norm_gain):
    num_blocks = TOKENS // BLOCK

    def to_blocks(matrix):
        return matrix.reshape(num_blocks, BLOCK, HEADS, HD)
    causal = lower_mask()[None]
    gain_heads = norm_gain.reshape(HEADS, HD)[None]
    full_width = HEADS * HD

    def forward_step(running, block_in):
        query_rows = block_in[0].astype(jnp.float32)
        key_rows = block_in[1].astype(jnp.float32)
        value_rows = block_in[2].astype(jnp.float32)
        grad_rows = block_in[3].astype(jnp.float32)
        scores = jnp.einsum('thd,shd->hts', query_rows, key_rows)
        attend = rounded(jnp.where(causal, scores, 0.0))
        prefix_kv = rounded(running)
        attn_out = jnp.einsum('hts,shd->thd', attend.astype(jnp.float32), value_rows)
        attn_out = attn_out + jnp.einsum('thd,hde->the', query_rows, prefix_kv.astype(jnp.float32))
        scaled = gain_heads * grad_rows
        square_sum = lax.optimization_barrier(jnp.sum(attn_out * attn_out, axis=(1, 2)))
        cross_sum = lax.optimization_barrier(jnp.sum(scaled * attn_out, axis=(1, 2)))
        inverse = lax.rsqrt(square_sum / full_width + epsilon)
        factor = inverse * inverse * inverse * cross_sum / full_width
        grad_out = (inverse[:, None, None] * scaled - attn_out * factor[:, None, None]).astype(jnp.bfloat16)
        running = running + jnp.einsum('shd,she->hde', key_rows, value_rows)
        return (running, (grad_out, prefix_kv))
    start_state = jnp.zeros((HEADS, HD, HD), jnp.float32)
    inputs_fwd = (to_blocks(queries), to_blocks(key_vectors), to_blocks(value_vectors), to_blocks(out_grad))
    _, (grad_blocks, prefix_blocks) = lax.scan(forward_step, start_state, inputs_fwd)

    def backward_step(running, block_in):
        query_rows = block_in[0].astype(jnp.float32)
        key_rows = block_in[1].astype(jnp.float32)
        value_rows = block_in[2].astype(jnp.float32)
        grad_rows = block_in[3].astype(jnp.float32)
        prefix_kv = block_in[4].astype(jnp.float32)
        suffix_qd = rounded(running).astype(jnp.float32)
        scores = jnp.einsum('thd,shd->hts', query_rows, key_rows)
        attend = rounded(jnp.where(causal, scores, 0.0)).astype(jnp.float32)
        mixed = jnp.einsum('thd,shd->hts', grad_rows, value_rows)
        mixed = rounded(jnp.where(causal, mixed, 0.0)).astype(jnp.float32)
        query_grad = jnp.einsum('hts,shd->thd', mixed, key_rows) + jnp.einsum('the,hde->thd', grad_rows, prefix_kv)
        key_grad = jnp.einsum('hts,thd->shd', mixed, query_rows) + jnp.einsum('shj,hij->shi', value_rows, suffix_qd)
        value_grad = jnp.einsum('hts,thd->shd', attend, grad_rows) + jnp.einsum('shi,hij->shj', key_rows, suffix_qd)
        running = running + jnp.einsum('thd,the->hde', query_rows, grad_rows)
        return (running, (query_grad.astype(jnp.bfloat16), key_grad.astype(jnp.bfloat16), value_grad.astype(jnp.bfloat16)))
    inputs_bwd = (to_blocks(queries), to_blocks(key_vectors), to_blocks(value_vectors), grad_blocks, prefix_blocks)
    _, (query_grad, key_grad, value_grad) = lax.scan(backward_step, start_state, inputs_bwd, reverse=True)
    return (query_grad.reshape(TOKENS, full_width), key_grad.reshape(TOKENS, full_width), value_grad.reshape(TOKENS, full_width))
```

```python
import functools

import jax
import jax.numpy as jnp
from jax import lax
from jax.experimental import pallas as pl
from jax.experimental.pallas import tpu as pltpu
from jax.sharding import PartitionSpec as P

HD = 128
BLOCK = 512
HALF = 256
NX = 4
NY = 8
NH = 16
ROWS = 1024
WIDTH = 256
FULL_WIDTH = 4096
PIECE = 2 * HD // NY

epsilon = 1e-05
MESH = pl.DeviceIdType.MESH
f32 = jnp.float32
bf16 = jnp.bfloat16


def dot(a, b, ca, cb):
    return lax.dot_general(a, b, (((ca,), (cb,)), ((), ())), preferred_element_type=f32)


def far_first(i, middle):
    return middle + ((i + 1) // 2) * (1 - 2 * (i % 2))


def body(
    q_hbm, k_hbm, v_hbm, g_hbm, gain_ref, qo_hbm, ko_hbm, vo_hbm,
    q, k, v, g, att, attn, go, kacc, vacc, qo, ko, vo, pfx, side,
    tot, got, row, cols, out, fin, part, parts,
    in_sem, out_sem, s1, r1, s2, r2, s3, r3, hs, hr,
):
    ctx = lax.axis_index("ctx")
    head = lax.axis_index("head")
    x = ctx // NY
    y = ctx % NY

    loads = [
        pltpu.make_async_copy(src, dst, in_sem.at[i])
        for i, (src, dst) in enumerate(((k_hbm, k), (v_hbm, v), (q_hbm, q), (g_hbm, g)))
    ]
    for load in loads:
        load.start()

    barrier = pltpu.get_barrier_semaphore()

    def greet_y(i, c):
        pl.semaphore_signal(
            barrier, inc=1, device_id=(x * NY + (y + i) % NY, head), device_id_type=MESH
        )
        return c

    def greet_x(i, c):
        pl.semaphore_signal(
            barrier, inc=1, device_id=(((x + i) % NX) * NY + y, head), device_id_type=MESH
        )
        return c

    def greet_h(i, c):
        pl.semaphore_signal(barrier, inc=1, device_id=(ctx, (head + i) % NH), device_id_type=MESH)
        return c

    lax.fori_loop(1, NY, greet_y, 0)
    lax.fori_loop(1, NX, greet_x, 0)
    lax.fori_loop(1, NH, greet_h, 0)

    def copy1(n, i):
        dy = far_first(i, NY // 2)
        to = (y + dy) % NY
        return pltpu.make_async_remote_copy(
            src_ref=tot.at[n, to], dst_ref=got.at[n, y],
            send_sem=s1.at[n, dy], recv_sem=r1.at[n, dy],
            device_id=(x * NY + to, head), device_id_type=MESH,
        )

    def copy2(n, i):
        dx = far_first(i, NX // 2)
        to = (x + dx) % NX
        return pltpu.make_async_remote_copy(
            src_ref=row.at[n], dst_ref=cols.at[n, x],
            send_sem=s2.at[n, dx], recv_sem=r2.at[n, dx],
            device_id=(to * NY + y, head), device_id_type=MESH,
        )

    def copy3(n, i):
        dy = far_first(i, NY // 2)
        to = (y + dy) % NY
        return pltpu.make_async_remote_copy(
            src_ref=out.at[n, to], dst_ref=fin.at[n, y],
            send_sem=s3.at[n, dy], recv_sem=r3.at[n, dy],
            device_id=(x * NY + to, head), device_id_type=MESH,
        )

    def copy_h(i):
        dh = far_first(i, NH // 2)
        return pltpu.make_async_remote_copy(
            src_ref=part, dst_ref=parts.at[head],
            send_sem=hs.at[dh], recv_sem=hr.at[dh],
            device_id=(ctx, (head + dh) % NH), device_id_type=MESH,
        )

    def start_all(count, copy):
        def step(i, c):
            copy(i).start()
            return c

        lax.fori_loop(0, count, step, 0)

    def wait_all(count, copy):
        def step(i, c):
            copy(i).wait()
            return c

        lax.fori_loop(0, count, step, 0)

    def scan_scatter(n):
        start_all(NY - 1, functools.partial(copy1, n))
        got[n, y] = tot[n, y]

    def scan_gather(n):
        wait_all(NY - 1, functools.partial(copy1, n))
        total = got[n, 0]
        for j in range(1, NY):
            total = total + got[n, j]
        row[n] = total
        start_all(NX - 1, functools.partial(copy2, n))
        cols[n, x] = total

    def scan_return(n):
        wait_all(NX - 1, functools.partial(copy2, n))
        running = jnp.zeros((PIECE, HD), f32)
        for j in range(NX):
            take = (j < x) if n == 0 else (j > x)
            running = running + jnp.where(take, cols[n, j], 0.0)
        for j in range(NY) if n == 0 else range(NY - 1, -1, -1):
            out[n, j] = running
            running = running + got[n, j]
        start_all(NY - 1, functools.partial(copy3, n))
        fin[n, y] = out[n, y]

    def scan_end(n):
        wait_all(NY - 1, functools.partial(copy3, n))

    def state(n, h):
        return fin[n, 4 * h : 4 * h + 4].reshape(HD, HD)

    diagonal = lax.broadcasted_iota(jnp.int32, (HALF, HALF), 0) >= lax.broadcasted_iota(
        jnp.int32, (HALF, HALF), 1
    )

    def masked(tile):
        return jnp.where(diagonal, tile, 0.0).astype(bf16)

    def block_of(b):
        return slice(b * BLOCK, (b + 1) * BLOCK)

    def cols_of(h):
        return slice(h * HD, (h + 1) * HD)

    loads[0].wait()
    loads[1].wait()
    for h in range(2):
        first = dot(k[block_of(0), cols_of(h)], v[block_of(0), cols_of(h)], 0, 0)
        second = dot(k[block_of(1), cols_of(h)], v[block_of(1), cols_of(h)], 0, 0)
        side[h] = first
        tot[0, 4 * h : 4 * h + 4] = (first + second).reshape(4, PIECE, HD)
    pl.semaphore_wait(barrier, (NY - 1) + (NX - 1) + (NH - 1))
    scan_scatter(0)

    def places(i):
        top = pl.multiple_of((i // 2) * BLOCK, BLOCK)
        col = pl.ds(pl.multiple_of((i % 2) * HD, HD), HD)
        return pl.ds(top, HALF), pl.ds(pl.multiple_of(top + HALF, HALF), HALF), col

    loads[2].wait()

    def inside(i, c):
        lo, hi, col = places(i)
        k0, k1, v0, v1 = k[lo, col], k[hi, col], v[lo, col], v[hi, col]
        a00 = masked(dot(q[lo, col], k0, 1, 1))
        a10 = dot(q[hi, col], k0, 1, 1).astype(bf16)
        a11 = masked(dot(q[hi, col], k1, 1, 1))
        att[i, 0] = a00
        att[i, 1] = a10
        att[i, 2] = a11
        attn[lo, col] = dot(a00, v0, 1, 0)
        attn[hi, col] = dot(a10, v0, 1, 0) + dot(a11, v1, 1, 0)
        return c

    lax.fori_loop(0, 4, inside, 0)
    loads[3].wait()
    scan_gather(0)
    scan_return(0)
    scan_end(0)

    for b in range(2):
        squares = jnp.zeros((BLOCK, HD), f32)
        crosses = jnp.zeros((BLOCK, HD), f32)
        for h in range(2):
            prefix = state(0, h)
            if b == 1:
                prefix = prefix + side[h]
            prefix = prefix.astype(bf16)
            pfx[2 * b + h] = prefix
            o = attn[block_of(b), cols_of(h)] + dot(q[block_of(b), cols_of(h)], prefix, 1, 0)
            attn[block_of(b), cols_of(h)] = o
            scaled = gain_ref[:, cols_of(h)] * g[block_of(b), cols_of(h)].astype(f32)
            squares = squares + o * o
            crosses = crosses + scaled * o
        square_row = jnp.sum(squares.T, axis=0, keepdims=True)
        cross_row = jnp.sum(crosses.T, axis=0, keepdims=True)
        for half in range(2):
            lanes = slice(half * HALF, (half + 1) * HALF)
            at = 2 * b + half
            part[at : at + 1, :] = square_row[:, lanes]
            part[4 + at : 5 + at, :] = cross_row[:, lanes]
    start_all(NH - 1, copy_h)
    parts[head] = part[...]
    wait_all(NH - 1, copy_h)
    sums = parts[0]
    for j in range(1, NH):
        sums = sums + parts[j]
    inverse = lax.rsqrt(sums[0:4] / FULL_WIDTH + epsilon)
    factor = inverse * inverse * inverse * sums[4:8] / FULL_WIDTH

    for at in range(4):
        rows = slice(at * HALF, (at + 1) * HALF)
        inverse_col = jnp.broadcast_to(inverse[at : at + 1], (HD, HALF)).T
        factor_col = jnp.broadcast_to(factor[at : at + 1], (HD, HALF)).T
        for h in range(2):
            scaled = gain_ref[:, cols_of(h)] * g[rows, cols_of(h)].astype(f32)
            go[rows, cols_of(h)] = (
                inverse_col * scaled - attn[rows, cols_of(h)] * factor_col
            ).astype(bf16)
    for h in range(2):
        first = dot(q[block_of(0), cols_of(h)], go[block_of(0), cols_of(h)], 0, 0)
        second = dot(q[block_of(1), cols_of(h)], go[block_of(1), cols_of(h)], 0, 0)
        side[h] = second
        tot[1, 4 * h : 4 * h + 4] = (first + second).reshape(4, PIECE, HD)
    scan_scatter(1)

    def gradients(i, c):
        lo, hi, col = places(i)
        q0, q1, k0, k1, v0, v1 = q[lo, col], q[hi, col], k[lo, col], k[hi, col], v[lo, col], v[hi, col]
        g0, g1 = go[lo, col], go[hi, col]
        prefix = pfx[i]
        m00 = masked(dot(g0, v0, 1, 1))
        m10 = dot(g1, v0, 1, 1).astype(bf16)
        m11 = masked(dot(g1, v1, 1, 1))
        qo[lo, col] = (dot(m00, k0, 1, 0) + dot(g0, prefix, 1, 1)).astype(bf16)
        qo[hi, col] = (dot(m10, k0, 1, 0) + dot(m11, k1, 1, 0) + dot(g1, prefix, 1, 1)).astype(bf16)
        kacc[lo, col] = dot(m00, q0, 0, 0) + dot(m10, q1, 0, 0)
        kacc[hi, col] = dot(m11, q1, 0, 0)
        vacc[lo, col] = dot(att[i, 0], g0, 0, 0) + dot(att[i, 1], g1, 0, 0)
        vacc[hi, col] = dot(att[i, 2], g1, 0, 0)
        return c

    lax.fori_loop(0, 4, gradients, 0)
    q_store = pltpu.make_async_copy(qo, qo_hbm, out_sem.at[0])
    q_store.start()
    scan_gather(1)
    scan_return(1)
    scan_end(1)

    for h in range(2):
        for b in range(2):
            suffix = state(1, h)
            if b == 0:
                suffix = suffix + side[h]
            suffix = suffix.astype(bf16)
            at = block_of(b), cols_of(h)
            ko[at] = (kacc[at] + dot(v[at], suffix, 1, 1)).astype(bf16)
            vo[at] = (vacc[at] + dot(k[at], suffix, 1, 0)).astype(bf16)
    k_store = pltpu.make_async_copy(ko, ko_hbm, out_sem.at[1])
    v_store = pltpu.make_async_copy(vo, vo_hbm, out_sem.at[2])
    k_store.start()
    v_store.start()
    q_store.wait()
    k_store.wait()
    v_store.wait()


def shards(queries, key_vectors, value_vectors, out_grad, norm_gain):
    tokens = pltpu.VMEM((ROWS, WIDTH), bf16)
    wide = pltpu.VMEM((ROWS, WIDTH), f32)
    pieces = pltpu.VMEM((2, NY, PIECE, HD), f32)
    any_space = pl.BlockSpec(memory_space=pl.ANY)
    sem = pltpu.SemaphoreType.DMA
    result = jax.ShapeDtypeStruct((ROWS, WIDTH), bf16)
    return pl.pallas_call(
        body,
        out_shape=(result, result, result),
        in_specs=[any_space] * 4 + [pl.BlockSpec(memory_space=pltpu.VMEM)],
        out_specs=[any_space] * 3,
        scratch_shapes=[
            tokens, tokens, tokens, tokens,
            pltpu.VMEM((4, 3, HALF, HALF), bf16),
            wide, tokens, wide, wide, tokens, tokens, tokens,
            pltpu.VMEM((4, HD, HD), bf16),
            pltpu.VMEM((2, HD, HD), f32),
            pieces, pieces,
            pltpu.VMEM((2, PIECE, HD), f32),
            pltpu.VMEM((2, NX, PIECE, HD), f32),
            pieces, pieces,
            pltpu.VMEM((8, HALF), f32),
            pltpu.VMEM((NH, 8, HALF), f32),
            sem((4,)), sem((3,)),
            sem((2, NY)), sem((2, NY)),
            sem((2, NX)), sem((2, NX)),
            sem((2, NY)), sem((2, NY)),
            sem((NH,)), sem((NH,)),
        ],
        compiler_params=pltpu.CompilerParams(collective_id=0, has_side_effects=True),
    )(queries, key_vectors, value_vectors, out_grad, norm_gain.reshape(1, WIDTH))


def solution(mesh):
    placed = (P("ctx", "head"), P("ctx", "head"), P("ctx", "head"), P("ctx", "head"), P("head"))
    return jax.shard_map(
        shards,
        mesh=mesh,
        in_specs=placed,
        out_specs=(P("ctx", "head"), P("ctx", "head"), P("ctx", "head")),
        check_vma=False,
    )
```

```python
import functools

import jax
import jax.numpy as jnp
from jax import lax
from jax.experimental import pallas as pl
from jax.experimental.pallas import tpu as pltpu
from jax.sharding import PartitionSpec as P

HD = 128
BLOCK = 512
HALF = 256
NX = 4
NY = 8
NH = 16
ROWS = 1024
WIDTH = 256
FULL_WIDTH = 4096
CHUNKS = 4
PIECE = 2 * HD // NY // CHUNKS
PER_HEAD = CHUNKS // 2

epsilon = 1e-05
MESH = pl.DeviceIdType.MESH
f32 = jnp.float32
bf16 = jnp.bfloat16


def dot(a, b, ca, cb):
    return lax.dot_general(a, b, (((ca,), (cb,)), ((), ())), preferred_element_type=f32)


def far_first(i, middle):
    return middle + ((i + 1) // 2) * (1 - 2 * (i % 2))


def body(
    q_hbm, k_hbm, v_hbm, g_hbm, gain_ref, qo, ko, vo,
    q, k, v, g, att, attn, go, kacc, vacc, pfx, side,
    tot, got, row, cols, out, fin, part, parts,
    in_sem, s1, r1, s2, r2, s3, r3, hs, hr,
):
    ctx = lax.axis_index("ctx")
    head = lax.axis_index("head")
    x = ctx // NY
    y = ctx % NY

    loads = [
        pltpu.make_async_copy(src, dst, in_sem.at[i])
        for i, (src, dst) in enumerate(((k_hbm, k), (v_hbm, v), (q_hbm, q), (g_hbm, g)))
    ]
    for load in loads:
        load.start()

    barrier = pltpu.get_barrier_semaphore()

    def greet_y(i, c):
        pl.semaphore_signal(
            barrier, inc=1, device_id=(x * NY + (y + i) % NY, head), device_id_type=MESH
        )
        return c

    def greet_x(i, c):
        pl.semaphore_signal(
            barrier, inc=1, device_id=(((x + i) % NX) * NY + y, head), device_id_type=MESH
        )
        return c

    def greet_h(i, c):
        pl.semaphore_signal(barrier, inc=1, device_id=(ctx, (head + i) % NH), device_id_type=MESH)
        return c

    lax.fori_loop(1, NY, greet_y, 0)
    lax.fori_loop(1, NX, greet_x, 0)
    lax.fori_loop(1, NH, greet_h, 0)

    def copy1(n, i):
        dy = far_first(i, NY // 2)
        to = (y + dy) % NY
        return pltpu.make_async_remote_copy(
            src_ref=tot.at[n, to], dst_ref=got.at[n, y],
            send_sem=s1.at[n, dy], recv_sem=r1.at[n, dy],
            device_id=(x * NY + to, head), device_id_type=MESH,
        )

    def copy2(n, i):
        dx = far_first(i, NX // 2)
        to = (x + dx) % NX
        return pltpu.make_async_remote_copy(
            src_ref=row.at[n], dst_ref=cols.at[n, x],
            send_sem=s2.at[n, dx], recv_sem=r2.at[n, dx],
            device_id=(to * NY + y, head), device_id_type=MESH,
        )

    def copy3(n, i):
        dy = far_first(i, NY // 2)
        to = (y + dy) % NY
        return pltpu.make_async_remote_copy(
            src_ref=out.at[n, to], dst_ref=fin.at[n, y],
            send_sem=s3.at[n, dy], recv_sem=r3.at[n, dy],
            device_id=(x * NY + to, head), device_id_type=MESH,
        )

    def copy_h(b, i):
        dh = far_first(i, NH // 2)
        return pltpu.make_async_remote_copy(
            src_ref=part.at[b], dst_ref=parts.at[b, head],
            send_sem=hs.at[b, dh], recv_sem=hr.at[b, dh],
            device_id=(ctx, (head + dh) % NH), device_id_type=MESH,
        )

    def start_all(count, copy):
        def step(i, c):
            copy(i).start()
            return c

        lax.fori_loop(0, count, step, 0)

    def wait_all(count, copy):
        def step(i, c):
            copy(i).wait()
            return c

        lax.fori_loop(0, count, step, 0)

    def scan_scatter(n):
        def step(c, _):
            at = n * CHUNKS + c
            start_all(NY - 1, functools.partial(copy1, at))
            got[at, y] = tot[at, y]
            return _

        lax.fori_loop(0, CHUNKS, step, 0)

    def scan_gather(n):
        def step(c, _):
            at = n * CHUNKS + c
            wait_all(NY - 1, functools.partial(copy1, at))
            total = got[at, 0]
            for j in range(1, NY):
                total = total + got[at, j]
            row[at] = total
            start_all(NX - 1, functools.partial(copy2, at))
            cols[at, x] = total
            return _

        lax.fori_loop(0, CHUNKS, step, 0)

    def scan_return(n):
        def step(c, _):
            at = n * CHUNKS + c
            wait_all(NX - 1, functools.partial(copy2, at))
            running = jnp.zeros((PIECE, HD), f32)
            for j in range(NX):
                take = (j < x) if n == 0 else (j > x)
                running = running + jnp.where(take, cols[at, j], 0.0)
            for j in range(NY) if n == 0 else range(NY - 1, -1, -1):
                out[at, j] = running
                running = running + got[at, j]
            start_all(NY - 1, functools.partial(copy3, at))
            fin[at, y] = out[at, y]
            return _

        lax.fori_loop(0, CHUNKS, step, 0)

    def scan_end(n, h):
        def step(c, _):
            wait_all(NY - 1, functools.partial(copy3, n * CHUNKS + h * PER_HEAD + c))
            return _

        lax.fori_loop(0, PER_HEAD, step, 0)

    def places_of(n, h):
        return slice(n * CHUNKS + h * PER_HEAD, n * CHUNKS + (h + 1) * PER_HEAD)

    def state(n, h):
        return fin[places_of(n, h)].reshape(HD, HD)

    def set_total(n, h, total):
        tot[places_of(n, h)] = total.reshape(PER_HEAD, NY, PIECE, HD)

    diagonal = lax.broadcasted_iota(jnp.int32, (HALF, HALF), 0) >= lax.broadcasted_iota(
        jnp.int32, (HALF, HALF), 1
    )

    def masked(tile):
        return jnp.where(diagonal, tile, 0.0).astype(bf16)

    def block_of(b):
        return slice(b * BLOCK, (b + 1) * BLOCK)

    def cols_of(h):
        return slice(h * HD, (h + 1) * HD)

    loads[0].wait()
    loads[1].wait()
    for h in range(2):
        first = dot(k[block_of(0), cols_of(h)], v[block_of(0), cols_of(h)], 0, 0)
        second = dot(k[block_of(1), cols_of(h)], v[block_of(1), cols_of(h)], 0, 0)
        side[h] = first
        set_total(0, h, first + second)
    pl.semaphore_wait(barrier, (NY - 1) + (NX - 1) + (NH - 1))
    scan_scatter(0)

    def places(i):
        top = pl.multiple_of((i // 2) * BLOCK, BLOCK)
        col = pl.ds(pl.multiple_of((i % 2) * HD, HD), HD)
        return pl.ds(top, HALF), pl.ds(pl.multiple_of(top + HALF, HALF), HALF), col

    loads[2].wait()

    def inside(i, c):
        lo, hi, col = places(i)
        k0, k1, v0, v1 = k[lo, col], k[hi, col], v[lo, col], v[hi, col]
        a00 = masked(dot(q[lo, col], k0, 1, 1))
        a10 = dot(q[hi, col], k0, 1, 1).astype(bf16)
        a11 = masked(dot(q[hi, col], k1, 1, 1))
        att[i, 0] = a00
        att[i, 1] = a10
        att[i, 2] = a11
        attn[lo, col] = dot(a00, v0, 1, 0)
        attn[hi, col] = dot(a10, v0, 1, 0) + dot(a11, v1, 1, 0)
        return c

    lax.fori_loop(0, 4, inside, 0)
    loads[3].wait()
    scan_gather(0)
    scan_return(0)

    for b in range(2):
        squares = jnp.zeros((BLOCK, HD), f32)
        crosses = jnp.zeros((BLOCK, HD), f32)
        for h in range(2):
            if b == 0:
                scan_end(0, h)
            prefix = state(0, h)
            if b == 1:
                prefix = prefix + side[h]
            prefix = prefix.astype(bf16)
            pfx[2 * b + h] = prefix
            o = attn[block_of(b), cols_of(h)] + dot(q[block_of(b), cols_of(h)], prefix, 1, 0)
            attn[block_of(b), cols_of(h)] = o
            scaled = gain_ref[:, cols_of(h)] * g[block_of(b), cols_of(h)].astype(f32)
            squares = squares + o * o
            crosses = crosses + scaled * o
        square_row = jnp.sum(squares.T, axis=0, keepdims=True)
        cross_row = jnp.sum(crosses.T, axis=0, keepdims=True)
        for half in range(2):
            lanes = slice(half * HALF, (half + 1) * HALF)
            part[b, half : half + 1, :] = square_row[:, lanes]
            part[b, 2 + half : 3 + half, :] = cross_row[:, lanes]
        start_all(NH - 1, functools.partial(copy_h, b))
        parts[b, head] = part[b]

    for b in range(2):
        wait_all(NH - 1, functools.partial(copy_h, b))
        sums = parts[b, 0]
        for j in range(1, NH):
            sums = sums + parts[b, j]
        inverse = lax.rsqrt(sums[0:2] / FULL_WIDTH + epsilon)
        factor = inverse * inverse * inverse * sums[2:4] / FULL_WIDTH
        for half in range(2):
            rows = slice(b * BLOCK + half * HALF, b * BLOCK + (half + 1) * HALF)
            inverse_col = jnp.broadcast_to(inverse[half : half + 1], (HD, HALF)).T
            factor_col = jnp.broadcast_to(factor[half : half + 1], (HD, HALF)).T
            for h in range(2):
                scaled = gain_ref[:, cols_of(h)] * g[rows, cols_of(h)].astype(f32)
                go[rows, cols_of(h)] = (
                    inverse_col * scaled - attn[rows, cols_of(h)] * factor_col
                ).astype(bf16)
    for h in range(2):
        first = dot(q[block_of(0), cols_of(h)], go[block_of(0), cols_of(h)], 0, 0)
        second = dot(q[block_of(1), cols_of(h)], go[block_of(1), cols_of(h)], 0, 0)
        side[h] = second
        set_total(1, h, first + second)
    scan_scatter(1)

    def gradients(i, c):
        lo, hi, col = places(i)
        q0, q1, k0, k1, v0, v1 = q[lo, col], q[hi, col], k[lo, col], k[hi, col], v[lo, col], v[hi, col]
        g0, g1 = go[lo, col], go[hi, col]
        prefix = pfx[i]
        m00 = masked(dot(g0, v0, 1, 1))
        m10 = dot(g1, v0, 1, 1).astype(bf16)
        m11 = masked(dot(g1, v1, 1, 1))
        qo[lo, col] = (dot(m00, k0, 1, 0) + dot(g0, prefix, 1, 1)).astype(bf16)
        qo[hi, col] = (dot(m10, k0, 1, 0) + dot(m11, k1, 1, 0) + dot(g1, prefix, 1, 1)).astype(bf16)
        kacc[lo, col] = dot(m00, q0, 0, 0) + dot(m10, q1, 0, 0)
        kacc[hi, col] = dot(m11, q1, 0, 0)
        vacc[lo, col] = dot(att[i, 0], g0, 0, 0) + dot(att[i, 1], g1, 0, 0)
        vacc[hi, col] = dot(att[i, 2], g1, 0, 0)
        return c

    lax.fori_loop(0, 4, gradients, 0)
    scan_gather(1)
    scan_return(1)

    for h in range(2):
        scan_end(1, h)
        for b in range(2):
            suffix = state(1, h)
            if b == 0:
                suffix = suffix + side[h]
            suffix = suffix.astype(bf16)
            at = block_of(b), cols_of(h)
            ko[at] = (kacc[at] + dot(v[at], suffix, 1, 1)).astype(bf16)
            vo[at] = (vacc[at] + dot(k[at], suffix, 1, 0)).astype(bf16)


def hand_out(qo, ko, vo, qo_hbm, ko_hbm, vo_hbm, sems):
    stores = [
        pltpu.make_async_copy(src, dst, sems.at[i])
        for i, (src, dst) in enumerate(((qo, qo_hbm), (ko, ko_hbm), (vo, vo_hbm)))
    ]
    for store in stores:
        store.start()
    for store in stores:
        store.wait()


def shards(queries, key_vectors, value_vectors, out_grad, norm_gain):
    tokens = pltpu.VMEM((ROWS, WIDTH), bf16)
    wide = pltpu.VMEM((ROWS, WIDTH), f32)
    pieces = pltpu.VMEM((2 * CHUNKS, NY, PIECE, HD), f32)
    in_hbm = pl.BlockSpec(memory_space=pltpu.HBM)
    sem = pltpu.SemaphoreType.DMA
    result = jax.ShapeDtypeStruct((ROWS, WIDTH), bf16)
    grads = pl.pallas_call(
        body,
        out_shape=(pltpu.VMEM((ROWS, WIDTH), bf16),) * 3,
        in_specs=[in_hbm] * 4 + [pl.BlockSpec(memory_space=pltpu.VMEM)],
        out_specs=[pl.BlockSpec(memory_space=pltpu.VMEM)] * 3,
        scratch_shapes=[
            tokens, tokens, tokens, tokens,
            pltpu.VMEM((4, 3, HALF, HALF), bf16),
            wide, tokens, wide, wide,
            pltpu.VMEM((4, HD, HD), bf16),
            pltpu.VMEM((2, HD, HD), f32),
            pieces, pieces,
            pltpu.VMEM((2 * CHUNKS, PIECE, HD), f32),
            pltpu.VMEM((2 * CHUNKS, NX, PIECE, HD), f32),
            pieces, pieces,
            pltpu.VMEM((2, 4, HALF), f32),
            pltpu.VMEM((2, NH, 4, HALF), f32),
            sem((4,)),
            sem((2 * CHUNKS, NY)), sem((2 * CHUNKS, NY)),
            sem((2 * CHUNKS, NX)), sem((2 * CHUNKS, NX)),
            sem((2 * CHUNKS, NY)), sem((2 * CHUNKS, NY)),
            sem((2, NH)), sem((2, NH)),
        ],
        compiler_params=pltpu.CompilerParams(
            collective_id=0, has_side_effects=True, vmem_limit_bytes=24 * 1024 * 1024
        ),
    )(queries, key_vectors, value_vectors, out_grad, norm_gain.reshape(1, WIDTH))
    return pl.pallas_call(
        hand_out,
        out_shape=(result, result, result),
        in_specs=[pl.BlockSpec(memory_space=pltpu.VMEM)] * 3,
        out_specs=[in_hbm] * 3,
        scratch_shapes=[sem((3,))],
        compiler_params=pltpu.CompilerParams(vmem_limit_bytes=4 * 1024 * 1024),
    )(*grads)


def solution(mesh):
    placed = (P("ctx", "head"), P("ctx", "head"), P("ctx", "head"), P("ctx", "head"), P("head"))
    return jax.shard_map(
        shards,
        mesh=mesh,
        in_specs=placed,
        out_specs=(P("ctx", "head"), P("ctx", "head"), P("ctx", "head")),
        check_vma=False,
    )
```

```python
import functools

import jax
import jax.numpy as jnp
from jax import lax
from jax.experimental import pallas as pl
from jax.experimental.pallas import tpu as pltpu
from jax.sharding import PartitionSpec as P

HD = 128
BLOCK = 512
HALF = 256
NX = 4
NY = 8
NZ = 8
ROWS = 1024
WIDTH = 256
FULL_WIDTH = 4096
CHUNKS = 1
PIECE = 2 * HD // NY // CHUNKS

epsilon = 1e-05
MESH = pl.DeviceIdType.MESH
f32 = jnp.float32
bf16 = jnp.bfloat16


def dot(a, b, ca, cb):
    return lax.dot_general(a, b, (((ca,), (cb,)), ((), ())), preferred_element_type=f32)


def far_first(i, middle):
    return middle + ((i + 1) // 2) * (1 - 2 * (i % 2))


def body(
    q_hbm, k_hbm, v_hbm, g_hbm, gain_hbm, qo, ko, vo,
    q, k, v, g, gain_ref, att, attn, go, kacc, vacc, pfx, side,
    tot, got, row, cols, out, fin, part, mate, chip, parts,
    in_sem, s1, r1, s2, r2, s3, r3, hs, hr,
):
    ctx = lax.axis_index("ctx")
    head = lax.axis_index("head")
    x = lax.div(ctx, NY)
    y = lax.rem(ctx, NY)

    loads = [
        pltpu.make_async_copy(src, dst, in_sem.at[i])
        for i, (src, dst) in enumerate(
            ((k_hbm, k), (v_hbm, v), (q_hbm, q), (g_hbm, g), (gain_hbm, gain_ref))
        )
    ]
    for load in loads:
        load.start()

    barrier = pltpu.get_barrier_semaphore()

    def greet_y(i, c):
        pl.semaphore_signal(
            barrier, inc=1, device_id=(x * NY + lax.rem(y + i, NY), head), device_id_type=MESH
        )
        return c

    def greet_x(i, c):
        pl.semaphore_signal(
            barrier, inc=1, device_id=(lax.rem(x + i, NX) * NY + y, head), device_id_type=MESH
        )
        return c

    def greet_h(i, c):
        pl.semaphore_signal(
            barrier, inc=1, device_id=(ctx, lax.rem(head + 2 * i, 2 * NZ)), device_id_type=MESH
        )
        return c

    lax.fori_loop(1, NY, greet_y, 0)
    lax.fori_loop(1, NX, greet_x, 0)
    lax.fori_loop(1, NZ, greet_h, 0)
    pl.semaphore_signal(
        barrier, inc=1, device_id=(ctx, head + 1 - 2 * lax.rem(head, 2)), device_id_type=MESH
    )

    def copy1(n, i):
        dy = far_first(i, NY // 2)
        to = lax.rem(y + dy, NY)
        return pltpu.make_async_remote_copy(
            src_ref=tot.at[n, to], dst_ref=got.at[n, y],
            send_sem=s1.at[n, dy], recv_sem=r1.at[n, dy],
            device_id=(x * NY + to, head), device_id_type=MESH,
        )

    def copy2(n, i):
        dx = far_first(i, NX // 2)
        to = lax.rem(x + dx, NX)
        return pltpu.make_async_remote_copy(
            src_ref=row.at[n], dst_ref=cols.at[n, x],
            send_sem=s2.at[n, dx], recv_sem=r2.at[n, dx],
            device_id=(to * NY + y, head), device_id_type=MESH,
        )

    def copy3(n, i):
        dy = far_first(i, NY // 2)
        to = lax.rem(y + dy, NY)
        return pltpu.make_async_remote_copy(
            src_ref=out.at[n, to], dst_ref=fin.at[n, y],
            send_sem=s3.at[n, dy], recv_sem=r3.at[n, dy],
            device_id=(x * NY + to, head), device_id_type=MESH,
        )

    z = lax.div(head, 2)
    core = lax.rem(head, 2)
    swap = pltpu.make_async_remote_copy(
        src_ref=part, dst_ref=mate, send_sem=hs.at[0], recv_sem=hr.at[0],
        device_id=(ctx, z * 2 + 1 - core), device_id_type=MESH,
    )

    def copy_h(i):
        dz = far_first(i, NZ // 2)
        return pltpu.make_async_remote_copy(
            src_ref=chip, dst_ref=parts.at[z], send_sem=hs.at[dz], recv_sem=hr.at[dz],
            device_id=(ctx, lax.rem(z + dz, NZ) * 2 + core), device_id_type=MESH,
        )

    def start_all(count, copy):
        for i in range(count):
            copy(i).start()

    def wait_all(count, copy):
        def step(i, c):
            copy(i).wait()
            return c

        lax.fori_loop(0, count, step, 0)

    def scan_scatter(n):
        def step(c, _):
            at = n * CHUNKS + c
            start_all(NY - 1, functools.partial(copy1, at))
            got[at, y] = tot[at, y]
            return _

        lax.fori_loop(0, CHUNKS, step, 0)

    def scan_gather(n):
        def step(c, _):
            at = n * CHUNKS + c
            wait_all(NY - 1, functools.partial(copy1, at))
            total = got[at, 0]
            for j in range(1, NY):
                total = total + got[at, j]
            row[at] = total
            start_all(NX - 1, functools.partial(copy2, at))
            cols[at, x] = total
            return _

        lax.fori_loop(0, CHUNKS, step, 0)

    def scan_return(n):
        def step(c, _):
            at = n * CHUNKS + c
            wait_all(NX - 1, functools.partial(copy2, at))
            running = jnp.zeros((PIECE, HD), f32)
            for j in range(NX):
                take = (j < x) if n == 0 else (j > x)
                running = running + jnp.where(take, cols[at, j], 0.0)
            for j in range(NY) if n == 0 else range(NY - 1, -1, -1):
                out[at, j] = running
                running = running + got[at, j]
            start_all(NY - 1, functools.partial(copy3, at))
            fin[at, y] = out[at, y]
            return _

        lax.fori_loop(0, CHUNKS, step, 0)

    def scan_end(n, h):
        for c in range(CHUNKS):
            if c * 2 // CHUNKS == h:
                wait_all(NY - 1, functools.partial(copy3, n * CHUNKS + c))

    def places_of(n, h):
        if CHUNKS == 1:
            return n, slice(NY // 2 * h, NY // 2 * (h + 1))
        return slice(n * CHUNKS + h * CHUNKS // 2, n * CHUNKS + (h + 1) * CHUNKS // 2)

    def state(n, h):
        return fin[places_of(n, h)].reshape(HD, HD)

    def set_total(n, h, total):
        at = places_of(n, h)
        tot[at] = total.reshape(tot[at].shape)

    diagonal = lax.broadcasted_iota(jnp.int32, (HALF, HALF), 0) >= lax.broadcasted_iota(
        jnp.int32, (HALF, HALF), 1
    )

    def masked(tile):
        return jnp.where(diagonal, tile, 0.0).astype(bf16)

    def block_of(b):
        return slice(b * BLOCK, (b + 1) * BLOCK)

    def cols_of(h):
        return slice(h * HD, (h + 1) * HD)

    loads[0].wait()
    loads[1].wait()
    for h in range(2):
        first = dot(k[block_of(0), cols_of(h)], v[block_of(0), cols_of(h)], 0, 0)
        second = dot(k[block_of(1), cols_of(h)], v[block_of(1), cols_of(h)], 0, 0)
        side[h] = first
        set_total(0, h, first + second)
    pl.semaphore_wait(barrier, (NY - 1) + (NX - 1) + NZ)
    scan_scatter(0)

    def places(i):
        top = pl.multiple_of((i // 2) * BLOCK, BLOCK)
        col = pl.ds(pl.multiple_of((i % 2) * HD, HD), HD)
        return pl.ds(top, HALF), pl.ds(pl.multiple_of(top + HALF, HALF), HALF), col

    loads[2].wait()

    def inside(i, c):
        lo, hi, col = places(i)
        k0, k1, v0, v1 = k[lo, col], k[hi, col], v[lo, col], v[hi, col]
        a00 = masked(dot(q[lo, col], k0, 1, 1))
        a10 = dot(q[hi, col], k0, 1, 1).astype(bf16)
        a11 = masked(dot(q[hi, col], k1, 1, 1))
        att[i, 0] = a00
        att[i, 1] = a10
        att[i, 2] = a11
        attn[lo, col] = dot(a00, v0, 1, 0)
        attn[hi, col] = dot(a10, v0, 1, 0) + dot(a11, v1, 1, 0)
        return c

    lax.fori_loop(0, 4, inside, 0)
    loads[3].wait()
    loads[4].wait()
    scan_gather(0)
    scan_return(0)

    for b in range(2):
        squares = jnp.zeros((BLOCK, HD), f32)
        crosses = jnp.zeros((BLOCK, HD), f32)
        for h in range(2):
            if b == 0:
                scan_end(0, h)
            prefix = state(0, h)
            if b == 1:
                prefix = prefix + side[h]
            prefix = prefix.astype(bf16)
            pfx[2 * b + h] = prefix
            o = attn[block_of(b), cols_of(h)] + dot(q[block_of(b), cols_of(h)], prefix, 1, 0)
            attn[block_of(b), cols_of(h)] = o
            scaled = gain_ref[:, cols_of(h)] * g[block_of(b), cols_of(h)].astype(f32)
            squares = squares + o * o
            crosses = crosses + scaled * o
        square_row = jnp.sum(squares.T, axis=0, keepdims=True)
        cross_row = jnp.sum(crosses.T, axis=0, keepdims=True)
        for half in range(2):
            lanes = slice(half * HALF, (half + 1) * HALF)
            part[b, half : half + 1, :] = square_row[:, lanes]
            part[b, 2 + half : 3 + half, :] = cross_row[:, lanes]
    swap.start()
    swap.wait()
    both = part[...] + mate[...]
    chip[...] = both
    start_all(NZ - 1, copy_h)
    parts[z] = both
    wait_all(NZ - 1, copy_h)
    total = parts[0]
    for j in range(1, NZ):
        total = total + parts[j]

    for b in range(2):
        sums = total[b]
        inverse = lax.rsqrt(sums[0:2] / FULL_WIDTH + epsilon)
        factor = inverse * inverse * inverse * sums[2:4] / FULL_WIDTH
        for half in range(2):
            rows = slice(b * BLOCK + half * HALF, b * BLOCK + (half + 1) * HALF)
            inverse_col = jnp.broadcast_to(inverse[half : half + 1], (HD, HALF)).T
            factor_col = jnp.broadcast_to(factor[half : half + 1], (HD, HALF)).T
            for h in range(2):
                scaled = gain_ref[:, cols_of(h)] * g[rows, cols_of(h)].astype(f32)
                go[rows, cols_of(h)] = (
                    inverse_col * scaled - attn[rows, cols_of(h)] * factor_col
                ).astype(bf16)
    for h in range(2):
        first = dot(q[block_of(0), cols_of(h)], go[block_of(0), cols_of(h)], 0, 0)
        second = dot(q[block_of(1), cols_of(h)], go[block_of(1), cols_of(h)], 0, 0)
        side[h] = second
        set_total(1, h, first + second)
    scan_scatter(1)

    def gradients(i, c):
        lo, hi, col = places(i)
        q0, q1, k0, k1, v0, v1 = q[lo, col], q[hi, col], k[lo, col], k[hi, col], v[lo, col], v[hi, col]
        g0, g1 = go[lo, col], go[hi, col]
        prefix = pfx[i]
        m00 = masked(dot(g0, v0, 1, 1))
        m10 = dot(g1, v0, 1, 1).astype(bf16)
        m11 = masked(dot(g1, v1, 1, 1))
        qo[lo, col] = (dot(m00, k0, 1, 0) + dot(g0, prefix, 1, 1)).astype(bf16)
        qo[hi, col] = (dot(m10, k0, 1, 0) + dot(m11, k1, 1, 0) + dot(g1, prefix, 1, 1)).astype(bf16)
        kacc[lo, col] = dot(m00, q0, 0, 0) + dot(m10, q1, 0, 0)
        kacc[hi, col] = dot(m11, q1, 0, 0)
        vacc[lo, col] = dot(att[i, 0], g0, 0, 0) + dot(att[i, 1], g1, 0, 0)
        vacc[hi, col] = dot(att[i, 2], g1, 0, 0)
        return c

    lax.fori_loop(0, 4, gradients, 0)
    scan_gather(1)
    scan_return(1)

    for h in range(2):
        scan_end(1, h)
        for b in range(2):
            suffix = state(1, h)
            if b == 0:
                suffix = suffix + side[h]
            suffix = suffix.astype(bf16)
            at = block_of(b), cols_of(h)
            ko[at] = (kacc[at] + dot(v[at], suffix, 1, 1)).astype(bf16)
            vo[at] = (vacc[at] + dot(k[at], suffix, 1, 0)).astype(bf16)


def hand_out(qo, ko, vo, qo_hbm, ko_hbm, vo_hbm, sems):
    stores = [
        pltpu.make_async_copy(src, dst, sems.at[i])
        for i, (src, dst) in enumerate(((qo, qo_hbm), (ko, ko_hbm), (vo, vo_hbm)))
    ]
    for store in stores:
        store.start()
    for store in stores:
        store.wait()


def shards(queries, key_vectors, value_vectors, out_grad, norm_gain):
    tokens = pltpu.VMEM((ROWS, WIDTH), bf16)
    wide = pltpu.VMEM((ROWS, WIDTH), f32)
    pieces = pltpu.VMEM((2 * CHUNKS, NY, PIECE, HD), f32)
    in_hbm = pl.BlockSpec(memory_space=pltpu.HBM)
    sem = pltpu.SemaphoreType.DMA
    result = jax.ShapeDtypeStruct((ROWS, WIDTH), bf16)
    grads = pl.pallas_call(
        body,
        out_shape=(pltpu.VMEM((ROWS, WIDTH), bf16),) * 3,
        in_specs=[in_hbm] * 5,
        out_specs=[pl.BlockSpec(memory_space=pltpu.VMEM)] * 3,
        scratch_shapes=[
            tokens, tokens, tokens, tokens,
            pltpu.VMEM((1, WIDTH), f32),
            pltpu.VMEM((4, 3, HALF, HALF), bf16),
            wide, tokens, wide, wide,
            pltpu.VMEM((4, HD, HD), bf16),
            pltpu.VMEM((2, HD, HD), f32),
            pieces, pieces,
            pltpu.VMEM((2 * CHUNKS, PIECE, HD), f32),
            pltpu.VMEM((2 * CHUNKS, NX, PIECE, HD), f32),
            pieces, pieces,
            pltpu.VMEM((2, 4, HALF), f32), pltpu.VMEM((2, 4, HALF), f32), pltpu.VMEM((2, 4, HALF), f32),
            pltpu.VMEM((NZ, 2, 4, HALF), f32),
            sem((5,)),
            sem((2 * CHUNKS, NY)), sem((2 * CHUNKS, NY)),
            sem((2 * CHUNKS, NX)), sem((2 * CHUNKS, NX)),
            sem((2 * CHUNKS, NY)), sem((2 * CHUNKS, NY)),
            sem((NZ,)), sem((NZ,)),
        ],
        compiler_params=pltpu.CompilerParams(
            collective_id=0, has_side_effects=True, vmem_limit_bytes=65_170_464
        ),
    )(queries, key_vectors, value_vectors, out_grad, norm_gain.reshape(1, WIDTH))
    return pl.pallas_call(
        hand_out,
        out_shape=(result, result, result),
        in_specs=[pl.BlockSpec(memory_space=pltpu.VMEM)] * 3,
        out_specs=[in_hbm] * 3,
        scratch_shapes=[sem((3,))],
        compiler_params=pltpu.CompilerParams(vmem_limit_bytes=4 * 1024 * 1024),
    )(*grads)


def solution(mesh):
    placed = (P("ctx", "head"), P("ctx", "head"), P("ctx", "head"), P("ctx", "head"), P("head"))
    return jax.shard_map(
        shards,
        mesh=mesh,
        in_specs=placed,
        out_specs=(P("ctx", "head"), P("ctx", "head"), P("ctx", "head")),
        check_vma=False,
    )
```

```python
import functools

import jax
import jax.numpy as jnp
from jax import lax
from jax.experimental import pallas as pl
from jax.experimental.pallas import tpu as pltpu
from jax.sharding import PartitionSpec as P

HD = 128
BLOCK = 512
HALF = 256
NX = 4
NY = 8
NZ = 8
ROWS = 1024
WIDTH = 256
FULL_WIDTH = 4096
CHUNKS = 1
PIECE = 2 * HD // NY // CHUNKS

epsilon = 1e-05
MESH = pl.DeviceIdType.MESH
f32 = jnp.float32
bf16 = jnp.bfloat16


def dot(a, b, ca, cb):
    return lax.dot_general(a, b, (((ca,), (cb,)), ((), ())), preferred_element_type=f32)


def far_first(i, middle):
    return middle + ((i + 1) // 2) * (1 - 2 * (i % 2))


def body(
    q_hbm, k_hbm, v_hbm, g_hbm, gain_hbm, qo, kacc, vacc, k, v, sfx,
    q, g, gain_ref, att, attn, go, pfx, side,
    tot, got, row, cols, out, fin, part, mate, chip, parts,
    in_sem, s1, r1, s2, r2, s3, r3, hs, hr,
):
    ctx = lax.axis_index("ctx")
    head = lax.axis_index("head")
    x = lax.div(ctx, NY)
    y = lax.rem(ctx, NY)

    loads = [
        pltpu.make_async_copy(src, dst, in_sem.at[i])
        for i, (src, dst) in enumerate(
            ((k_hbm, k), (v_hbm, v), (q_hbm, q), (g_hbm, g), (gain_hbm, gain_ref))
        )
    ]

    barrier = pltpu.get_barrier_semaphore()

    def greet_y(i, c):
        pl.semaphore_signal(
            barrier, inc=1, device_id=(x * NY + lax.rem(y + i, NY), head), device_id_type=MESH
        )
        return c

    def greet_x(i, c):
        pl.semaphore_signal(
            barrier, inc=1, device_id=(lax.rem(x + i, NX) * NY + y, head), device_id_type=MESH
        )
        return c

    def greet_h(i, c):
        pl.semaphore_signal(
            barrier, inc=1, device_id=(ctx, lax.rem(head + 2 * i, 2 * NZ)), device_id_type=MESH
        )
        return c

    for i in range(1, NY):
        greet_y(i, 0)
    for i in range(1, NX):
        greet_x(i, 0)
    for i in range(1, NZ):
        greet_h(i, 0)
    pl.semaphore_signal(
        barrier, inc=1, device_id=(ctx, head + 1 - 2 * lax.rem(head, 2)), device_id_type=MESH
    )

    for load in loads:
        load.start()

    def copy1(n, i):
        dy = far_first(i, NY // 2)
        to = lax.rem(y + dy, NY)
        return pltpu.make_async_remote_copy(
            src_ref=tot.at[n, to], dst_ref=got.at[n, y],
            send_sem=s1.at[n, dy], recv_sem=r1.at[n, dy],
            device_id=(x * NY + to, head), device_id_type=MESH,
        )

    def copy2(n, i):
        dx = far_first(i, NX // 2)
        to = lax.rem(x + dx, NX)
        return pltpu.make_async_remote_copy(
            src_ref=row.at[n], dst_ref=cols.at[n, x],
            send_sem=s2.at[n, dx], recv_sem=r2.at[n, dx],
            device_id=(to * NY + y, head), device_id_type=MESH,
        )

    def copy3(n, i):
        dy = far_first(i, NY // 2)
        to = lax.rem(y + dy, NY)
        return pltpu.make_async_remote_copy(
            src_ref=out.at[n, to], dst_ref=fin.at[n, y],
            send_sem=s3.at[n, dy], recv_sem=r3.at[n, dy],
            device_id=(x * NY + to, head), device_id_type=MESH,
        )

    z = lax.div(head, 2)
    core = lax.rem(head, 2)
    swap = pltpu.make_async_remote_copy(
        src_ref=part, dst_ref=mate, send_sem=hs.at[0], recv_sem=hr.at[0],
        device_id=(ctx, z * 2 + 1 - core), device_id_type=MESH,
    )

    def copy_h(i):
        dz = far_first(i, NZ // 2)
        return pltpu.make_async_remote_copy(
            src_ref=chip, dst_ref=parts.at[z], send_sem=hs.at[dz], recv_sem=hr.at[dz],
            device_id=(ctx, lax.rem(z + dz, NZ) * 2 + core), device_id_type=MESH,
        )

    def start_all(count, copy):
        for i in range(count):
            copy(i).start()

    def wait_all(count, copy):
        for i in range(count):
            copy(i).wait()

    def scan_scatter(n):
        def step(c, _):
            at = n * CHUNKS + c
            start_all(NY - 1, functools.partial(copy1, at))
            got[at, y] = tot[at, y]
            return _

        lax.fori_loop(0, CHUNKS, step, 0)

    def scan_gather(n):
        def step(c, _):
            at = n * CHUNKS + c
            wait_all(NY - 1, functools.partial(copy1, at))
            total = got[at, 0]
            for j in range(1, NY):
                total = total + got[at, j]
            row[at] = total
            start_all(NX - 1, functools.partial(copy2, at))
            cols[at, x] = total
            return _

        lax.fori_loop(0, CHUNKS, step, 0)

    def scan_return(n):
        def step(c, _):
            at = n * CHUNKS + c
            wait_all(NX - 1, functools.partial(copy2, at))
            running = jnp.zeros((PIECE, HD), f32)
            for j in range(NX):
                take = (j < x) if n == 0 else (j > x)
                running = running + jnp.where(take, cols[at, j], 0.0)
            for j in range(NY) if n == 0 else range(NY - 1, -1, -1):
                out[at, j] = running
                running = running + got[at, j]
            start_all(NY - 1, functools.partial(copy3, at))
            fin[at, y] = out[at, y]
            return _

        lax.fori_loop(0, CHUNKS, step, 0)

    def scan_end(n, h):
        for c in range(CHUNKS):
            if c * 2 // CHUNKS == h:
                wait_all(NY - 1, functools.partial(copy3, n * CHUNKS + c))

    def places_of(n, h):
        if CHUNKS == 1:
            return n, slice(NY // 2 * h, NY // 2 * (h + 1))
        return slice(n * CHUNKS + h * CHUNKS // 2, n * CHUNKS + (h + 1) * CHUNKS // 2)

    def state(n, h):
        return fin[places_of(n, h)].reshape(HD, HD)

    def set_total(n, h, total):
        at = places_of(n, h)
        tot[at] = total.reshape(tot[at].shape)

    diagonal = lax.broadcasted_iota(jnp.int32, (HALF, HALF), 0) >= lax.broadcasted_iota(
        jnp.int32, (HALF, HALF), 1
    )

    def masked(tile):
        return jnp.where(diagonal, tile, 0.0).astype(bf16)

    def block_of(b):
        return slice(b * BLOCK, (b + 1) * BLOCK)

    def cols_of(h):
        return slice(h * HD, (h + 1) * HD)

    loads[0].wait()
    loads[1].wait()
    for h in range(2):
        first = dot(k[block_of(0), cols_of(h)], v[block_of(0), cols_of(h)], 0, 0)
        second = dot(k[block_of(1), cols_of(h)], v[block_of(1), cols_of(h)], 0, 0)
        side[h] = first
        set_total(0, h, first + second)
    pl.semaphore_wait(barrier, (NY - 1) + (NX - 1) + NZ)
    scan_scatter(0)

    def places(i):
        top = pl.multiple_of((i // 2) * BLOCK, BLOCK)
        col = pl.ds(pl.multiple_of((i % 2) * HD, HD), HD)
        return pl.ds(top, HALF), pl.ds(pl.multiple_of(top + HALF, HALF), HALF), col

    loads[2].wait()

    def inside(i, c):
        lo, hi, col = places(i)
        k0, k1, v0, v1 = k[lo, col], k[hi, col], v[lo, col], v[hi, col]
        a00 = masked(dot(q[lo, col], k0, 1, 1))
        a10 = dot(q[hi, col], k0, 1, 1).astype(bf16)
        a11 = masked(dot(q[hi, col], k1, 1, 1))
        att[i, 0] = a00
        att[i, 1] = a10
        att[i, 2] = a11
        attn[lo, col] = dot(a00, v0, 1, 0)
        attn[hi, col] = dot(a10, v0, 1, 0) + dot(a11, v1, 1, 0)
        return c

    lax.fori_loop(0, 4, inside, 0)
    loads[3].wait()
    loads[4].wait()
    scan_gather(0)
    scan_return(0)

    for b in range(2):
        squares = jnp.zeros((BLOCK, HD), f32)
        crosses = jnp.zeros((BLOCK, HD), f32)
        for h in range(2):
            if b == 0:
                scan_end(0, h)
            prefix = state(0, h)
            if b == 1:
                prefix = prefix + side[h]
            prefix = prefix.astype(bf16)
            pfx[2 * b + h] = prefix
            o = attn[block_of(b), cols_of(h)] + dot(q[block_of(b), cols_of(h)], prefix, 1, 0)
            attn[block_of(b), cols_of(h)] = o
            scaled = gain_ref[:, cols_of(h)] * g[block_of(b), cols_of(h)].astype(f32)
            squares = squares + o * o
            crosses = crosses + scaled * o
        square_row = jnp.sum(squares.T, axis=0, keepdims=True)
        cross_row = jnp.sum(crosses.T, axis=0, keepdims=True)
        for half in range(2):
            lanes = slice(half * HALF, (half + 1) * HALF)
            part[b, half : half + 1, :] = square_row[:, lanes]
            part[b, 2 + half : 3 + half, :] = cross_row[:, lanes]
    swap.start()
    swap.wait()
    both = part[...] + mate[...]
    chip[...] = both
    start_all(NZ - 1, copy_h)
    parts[z] = both
    wait_all(NZ - 1, copy_h)
    total = parts[0]
    for j in range(1, NZ):
        total = total + parts[j]

    for b in range(2):
        sums = total[b]
        inverse = lax.rsqrt(sums[0:2] / FULL_WIDTH + epsilon)
        factor = inverse * inverse * inverse * sums[2:4] / FULL_WIDTH
        for half in range(2):
            rows = slice(b * BLOCK + half * HALF, b * BLOCK + (half + 1) * HALF)
            inverse_col = jnp.broadcast_to(inverse[half : half + 1], (HD, HALF)).T
            factor_col = jnp.broadcast_to(factor[half : half + 1], (HD, HALF)).T
            for h in range(2):
                scaled = gain_ref[:, cols_of(h)] * g[rows, cols_of(h)].astype(f32)
                go[rows, cols_of(h)] = (
                    inverse_col * scaled - attn[rows, cols_of(h)] * factor_col
                ).astype(bf16)
    for h in range(2):
        first = dot(q[block_of(0), cols_of(h)], go[block_of(0), cols_of(h)], 0, 0)
        second = dot(q[block_of(1), cols_of(h)], go[block_of(1), cols_of(h)], 0, 0)
        side[h] = second
        set_total(1, h, first + second)
    scan_scatter(1)

    def gradients(i, c):
        lo, hi, col = places(i)
        q0, q1, k0, k1, v0, v1 = q[lo, col], q[hi, col], k[lo, col], k[hi, col], v[lo, col], v[hi, col]
        g0, g1 = go[lo, col], go[hi, col]
        prefix = pfx[i]
        m00 = masked(dot(g0, v0, 1, 1))
        m10 = dot(g1, v0, 1, 1).astype(bf16)
        m11 = masked(dot(g1, v1, 1, 1))
        qo[lo, col] = (dot(m00, k0, 1, 0) + dot(g0, prefix, 1, 1)).astype(bf16)
        qo[hi, col] = (dot(m10, k0, 1, 0) + dot(m11, k1, 1, 0) + dot(g1, prefix, 1, 1)).astype(bf16)
        kacc[lo, col] = dot(m00, q0, 0, 0) + dot(m10, q1, 0, 0)
        kacc[hi, col] = dot(m11, q1, 0, 0)
        vacc[lo, col] = dot(att[i, 0], g0, 0, 0) + dot(att[i, 1], g1, 0, 0)
        vacc[hi, col] = dot(att[i, 2], g1, 0, 0)
        return c

    lax.fori_loop(0, 4, gradients, 0)
    scan_gather(1)
    scan_return(1)

    for h in range(2):
        scan_end(1, h)
        suffix = state(1, h)
        sfx[2 + h] = suffix.astype(bf16)
        sfx[h] = (suffix + side[h]).astype(bf16)


def last(qo, kacc, vacc, k, v, sfx, qo_hbm, ko_hbm, vo_hbm, ko, vo, sems):
    store = pltpu.make_async_copy(qo, qo_hbm, sems.at[4])
    store.start()
    stores = [store]
    for b in range(2):
        rows = slice(b * BLOCK, (b + 1) * BLOCK)
        for h in range(2):
            at = rows, slice(h * HD, (h + 1) * HD)
            suffix = sfx[2 * b + h]
            ko[at] = (kacc[at] + dot(v[at], suffix, 1, 1)).astype(bf16)
            vo[at] = (vacc[at] + dot(k[at], suffix, 1, 0)).astype(bf16)
        for i, (src, dst) in enumerate(((ko, ko_hbm), (vo, vo_hbm))):
            store = pltpu.make_async_copy(src.at[rows], dst.at[rows], sems.at[2 * b + i])
            store.start()
            stores.append(store)
    for store in stores:
        store.wait()


def shards(queries, key_vectors, value_vectors, out_grad, norm_gain):
    tokens = pltpu.VMEM((ROWS, WIDTH), bf16)
    wide = pltpu.VMEM((ROWS, WIDTH), f32)
    pieces = pltpu.VMEM((2 * CHUNKS, NY, PIECE, HD), f32)
    in_hbm = pl.BlockSpec(memory_space=pltpu.HBM)
    sem = pltpu.SemaphoreType.DMA
    result = jax.ShapeDtypeStruct((ROWS, WIDTH), bf16)
    grads = pl.pallas_call(
        body,
        out_shape=(tokens, wide, wide, tokens, tokens, pltpu.VMEM((4, HD, HD), bf16)),
        in_specs=[in_hbm] * 5,
        out_specs=[pl.BlockSpec(memory_space=pltpu.VMEM)] * 6,
        scratch_shapes=[
            tokens, tokens,
            pltpu.VMEM((1, WIDTH), f32),
            pltpu.VMEM((4, 3, HALF, HALF), bf16),
            wide, tokens,
            pltpu.VMEM((4, HD, HD), bf16),
            pltpu.VMEM((2, HD, HD), f32),
            pieces, pieces,
            pltpu.VMEM((2 * CHUNKS, PIECE, HD), f32),
            pltpu.VMEM((2 * CHUNKS, NX, PIECE, HD), f32),
            pieces, pieces,
            pltpu.VMEM((2, 4, HALF), f32), pltpu.VMEM((2, 4, HALF), f32), pltpu.VMEM((2, 4, HALF), f32),
            pltpu.VMEM((NZ, 2, 4, HALF), f32),
            sem((5,)),
            sem((2 * CHUNKS, NY)), sem((2 * CHUNKS, NY)),
            sem((2 * CHUNKS, NX)), sem((2 * CHUNKS, NX)),
            sem((2 * CHUNKS, NY)), sem((2 * CHUNKS, NY)),
            sem((NZ,)), sem((NZ,)),
        ],
        compiler_params=pltpu.CompilerParams(
            collective_id=0, has_side_effects=True, vmem_limit_bytes=62_900_000
        ),
    )(queries, key_vectors, value_vectors, out_grad, norm_gain.reshape(1, WIDTH))
    return pl.pallas_call(
        last,
        out_shape=(result, result, result),
        in_specs=[pl.BlockSpec(memory_space=pltpu.VMEM)] * 6,
        out_specs=[in_hbm] * 3,
        scratch_shapes=[tokens, tokens, sem((5,))],
        compiler_params=pltpu.CompilerParams(vmem_limit_bytes=4 * 1024 * 1024),
    )(*grads)


def solution(mesh):
    placed = (P("ctx", "head"), P("ctx", "head"), P("ctx", "head"), P("ctx", "head"), P("head"))
    return jax.shard_map(
        shards,
        mesh=mesh,
        in_specs=placed,
        out_specs=(P("ctx", "head"), P("ctx", "head"), P("ctx", "head")),
        check_vma=False,
    )
```
